32 devices in a mesh: freq: 8 (over z, x), panel: 4 (over y, core).
Axes of the slice: x: 2, y: 2, z: 4, core: 2. Of those that a mesh axis runs over, the one named last changes fastest.
Arguments:
- wavefield: float32 [8, 2, 128, 4096], P('freq', None, None, 'panel'), may hold values from -6 to 6
- direct: float32 [8, 2, 128, 4096], P('freq', None, None, 'panel'), may hold values from -6 to 6
- left_factors: float32 [8, 4096, 6, 128], P('freq', 'panel'), may hold values from -0.375 to 0.375
- right_factors: float32 [8, 16, 6, 256, 128], P('freq', 'panel'), may hold values from -0.3125 to 0.3125
- tile_src: int32 [16, 6], P('panel'), may hold values from -1 to 7, as said below
- onset: int32 [128, 2048], P('freq'), may hold values from 128 to 895
Outputs:
- focusing: float32 [8, 2, 128, 4096], P('freq', None, None, 'panel')
The draws below stay inside these ranges and needn't reach their ends.
Inputs may be any that keep to these rules, and one draw needn't show every extreme that they name: `tile_src`: in each receiver panel's row the first k slots name distinct source tiles, with 2 <= k <= 6, and the other slots hold -1; in every aligned block of 4 panels at least one panel fills all 6 slots.
All inputs are finite; a program needn't handle non-finite values.
Results may differ from the reference program's by a relative error of at most 0.0003.
Values sent between devices are 32-bit elements; how exact they have to be, the bound alone decides.
A program may use at most 128 MiB of HBM per device.

```python
import math
import jax
import jax.numpy as jnp
from jax import lax

TILE = 256
RANK = 64
SRC_TILES = 8
SLOTS = 6
VS = 128
NT = 1024
FIRST_BIN = 8
RP_DEV = 4
PANELS = 16
RECV = 4096
SRC = 2048
NF = 8


def draw_tile_src(key, part):
    key_order = jax.random.fold_in(key, 11)
    key_count = jax.random.fold_in(key, 23)
    key_full = jax.random.fold_in(key, 37)
    scores = jax.random.randint(key_order, (PANELS, SRC_TILES), 0, 1 << 20) * SRC_TILES + jnp.arange(SRC_TILES, dtype=jnp.int32)[None, :]
    order = jnp.argsort(scores, axis=1).astype(jnp.int32)[:, :SLOTS]
    counts = jax.random.randint(key_count, (PANELS,), 2, SLOTS + 1)
    full_at = jax.random.randint(key_full, (PANELS // RP_DEV,), 0, RP_DEV)
    position = jnp.arange(PANELS, dtype=jnp.int32) % RP_DEV
    counts = jnp.where(position == jnp.repeat(full_at, RP_DEV), SLOTS, counts)
    slot_index = jnp.arange(SLOTS, dtype=jnp.int32)
    return jnp.where(slot_index[None, :] < counts[:, None], order, -1).astype(jnp.int32)


def set_ends(values, own_key, smallest, top_value):
    extent = values.shape
    index_at = [jax.random.randint(jax.random.fold_in(own_key, axis), (), 0, extent[axis]) for axis in range(len(extent))]
    values = values.at[tuple(index_at)].set(smallest)
    longest = extent.index(max(extent))
    index_at[longest] = (index_at[longest] + 1) % extent[longest]
    return values.at[tuple(index_at)].set(top_value)


def shard_levels(rng, shape, pieces, least, top_value):
    factor_of, own = 1.0, jax.random.fold_in(rng, 6)
    for dim, blocks in pieces:
        draws = jnp.exp(jax.random.uniform(jax.random.fold_in(own, dim), (blocks,), jnp.float32, least / len(pieces), top_value / len(pieces)))
        factor_of = factor_of * jnp.repeat(draws, shape[dim] // blocks).reshape([-1 if axis == dim else 1 for axis in range(len(shape))])
    return factor_of


def centred(own_key, shape, spread, most, pieces=(), kind=jnp.bfloat16):
    drawn = spread * jax.random.normal(own_key, shape, jnp.float32)
    if pieces:
        drawn = drawn * shard_levels(own_key, shape, pieces, -0.22, 0.18)
    return jnp.clip(drawn, -most, most).astype(kind)


def setup_inputs(seed: int = 0) -> dict:
    key_of = jax.random.split(jax.random.key(seed), 7)
    wavefield = centred(key_of[0], (NF, 2, VS, RECV), 1.0, 6.0, ((0, 8), (3, 4)), jnp.float32)
    direct = centred(key_of[1], (NF, 2, VS, RECV), 1.0, 6.0, ((0, 8), (3, 4)), jnp.float32)
    left_factors = centred(key_of[2], (NF, RECV, SLOTS, 2 * RANK), TILE ** -0.5, 0.375, ((0, 8), (1, 4)), jnp.float32)
    right_factors = centred(key_of[3], (NF, PANELS, SLOTS, TILE, 2 * RANK), (RANK * SLOTS) ** -0.5, 0.3125, ((0, 8), (1, 4)), jnp.float32)
    tile_src = draw_tile_src(jax.random.fold_in(key_of[6], 71), 0)
    onset = set_ends(jax.random.randint(key_of[5], (VS, SRC), NT // 8, NT - NT // 8), jax.random.fold_in(key_of[5], 1), NT // 8, (NT - NT // 8) - 1).astype(jnp.int32)
    return {"wavefield": wavefield, "direct": direct, "left_factors": left_factors, "right_factors": right_factors, "tile_src": tile_src, "onset": onset}


HIGH = lax.Precision.HIGHEST

def pair_coef(products):
    half = products.shape[3] // 2
    real_part = products[0, :, :, :half] + products[1, :, :, half:]
    imag_part = products[1, :, :, :half] - products[0, :, :, half:]
    return jnp.stack([jnp.concatenate([real_part, -imag_part], axis=2), jnp.concatenate([imag_part, real_part], axis=2)])

def tile_adjoint(left, right, field, picks):
    products = jnp.einsum('ptsk,cvpt->cpskv', left, field, precision=HIGH)
    contrib = jnp.einsum('pstk,cpskv->cpstv', right, pair_coef(products), precision=HIGH)
    return jnp.einsum('psj,cpstv->cvjt', picks, contrib, precision=HIGH)

def tile_forward(left, right, source_field, picks):
    chosen = jnp.einsum('psj,cvjt->cpsvt', picks, source_field, precision=HIGH)
    products = jnp.einsum('pstk,cpsvt->cpskv', right, chosen, precision=HIGH)
    return jnp.einsum('ptsk,cpskv->cvpt', left, pair_coef(products), precision=HIGH)

def time_tables(count, length):
    times = jnp.arange(length, dtype=jnp.int32)
    freqs = jnp.arange(count, dtype=jnp.int32) + FIRST_BIN
    phase = freqs[None, :] * times[:, None] % length
    angle = 2.0 * math.pi / length * phase.astype(jnp.float32)
    waves = jnp.stack([jnp.cos(angle), -jnp.sin(angle)], axis=2).reshape(length, 2 * count)
    return (waves * (1.0 / math.sqrt(count)), waves.T * (1.0 / math.sqrt(length)))

def gate_block(block, marks, into, outof):
    count = block.shape[0]
    width = block.shape[2]
    length = into.shape[0]
    traces = jnp.dot(into, block.reshape(2 * count, width), precision=HIGH, preferred_element_type=jnp.float32)
    times = jnp.arange(length, dtype=jnp.int32)
    gated = jnp.where(times[:, None] < marks[None, :], traces, jnp.zeros_like(traces))
    back = jnp.dot(outof, gated, precision=HIGH, preferred_element_type=jnp.float32)
    return back.reshape(count, 2, width)

def apply_gate(moved, marks, into, outof):
    items = jnp.moveaxis(moved, 2, 0)
    result = lax.map(lambda pair: gate_block(pair[0], pair[1], into, outof), (items, marks))
    return jnp.moveaxis(result, 0, 2)

def reference(wavefield, direct, left_factors, right_factors, tile_src, onset):
    picks = (tile_src[:, :, None] == jnp.arange(SRC_TILES, dtype=jnp.int32)[None, None, :]).astype(jnp.float32)

    def adjoint_one(args):
        field, left, right = args
        left4 = left.reshape(PANELS, TILE, SLOTS, 2 * RANK)
        field4 = field.reshape(2, VS, PANELS, TILE)
        return tile_adjoint(left4, right, field4, picks).reshape(2, VS, SRC)
    adjoint = lax.map(adjoint_one, (wavefield, left_factors, right_factors))
    into, outof = time_tables(NF, NT)
    back = apply_gate(adjoint, onset, into, outof)

    def forward_one(args):
        source_field, left, right = args
        left4 = left.reshape(PANELS, TILE, SLOTS, 2 * RANK)
        result = tile_forward(left4, right, source_field.reshape(2, VS, SRC_TILES, TILE), picks)
        return result.reshape(2, VS, RECV)
    forward = lax.map(forward_one, (back, left_factors, right_factors))
    return direct - forward
```

```python
import functools
import math

import jax
import jax.numpy as jnp
from jax import lax
from jax.experimental import pallas as pl
from jax.experimental.pallas import tpu as pltpu
from jax.sharding import PartitionSpec as P

NT = 1024
FIRST_BIN = 8
SRC_TILES = 8
LANES = 128
BF16 = jnp.bfloat16
F32 = jnp.float32
NN = (((1,), (0,)), ((), ()))
NT_DIMS = (((1,), (1,)), ((), ()))


def split(x):
    high = x.astype(BF16)
    return high, (x - high.astype(F32)).astype(BF16)


def mxu(a, b, dims):
    return lax.dot_general(a, b, dims, preferred_element_type=F32)


def lanes(*parts):
    return jnp.concatenate(parts, axis=1)


def pair_coef(products):
    rows, width = products.shape
    first, second = products[: rows // 2], products[rows // 2 :]
    lane = lax.broadcasted_iota(jnp.int32, first.shape, 1)
    sign = jnp.where(lane < width // 2, 1.0, -1.0).astype(F32)
    swap = lambda x: pltpu.roll(x, width // 2, 1)
    return jnp.concatenate([first + sign * swap(second), second - sign * swap(first)], axis=0)


def adjoint_kernel(share, tile_ref, field_ref, left_ref, right_ref, onset_ref, out_ref, trig_ref):
    p = pl.program_id(0)
    slots, rows, width = left_ref.shape

    @pl.when(p == 0)
    def _():
        out_ref[...] = jnp.zeros_like(out_ref)
        start = lax.axis_index("panel") * share
        for c in range(share // LANES):
            at = pl.multiple_of(start + c * LANES, LANES)
            mark = onset_ref[:, pl.ds(at, LANES)]
            angle = (2.0 * math.pi / NT) * (mark & (NT - 1)).astype(F32)
            trig_ref[0, c] = jnp.cos(angle)
            trig_ref[1, c] = jnp.sin(angle)
            trig_ref[2, c] = mark.astype(F32)

    field = field_ref[...].reshape(-1, rows)
    fh, fl = split(field)
    for s in range(0, slots, 2):

        @pl.when(tile_ref[p, s] >= 0)
        def _(s=s):
            lh0, ll0 = split(left_ref[s])
            lh1, ll1 = split(left_ref[s + 1])
            lh, ll = lanes(lh0, lh1), lanes(ll0, ll1)
            products = mxu(fh, lh, NN) + mxu(fh, ll, NN) + mxu(fl, lh, NN)
            for i in range(2):
                ch, cl = split(pair_coef(products[:, i * width : (i + 1) * width]))
                rh, rl = split(right_ref[0, s + i])
                contrib = mxu(lanes(ch, cl, ch), lanes(rh, rh, rl), NT_DIMS)
                j = tile_ref[p, s + i]

                @pl.when(j >= 0)
                def _(j=j, contrib=contrib):
                    for b in range(rows // LANES):
                        out_ref[j * (rows // LANES) + b] += contrib[:, b * LANES : (b + 1) * LANES]


def forward_kernel(tile_ref, source_ref, direct_ref, left_ref, right_ref, out_ref):
    p = pl.program_id(0)
    slots, rows, width = left_ref.shape
    blocks = rows // LANES
    out_ref[...] = direct_ref[...]
    for s in range(0, slots, 2):

        @pl.when(tile_ref[p, s] >= 0)
        def _(s=s):
            highs, lows = [], []
            for i in range(2):
                j = tile_ref[p, s + i]
                at = jnp.maximum(j, 0)
                chosen = lanes(*[source_ref[at * blocks + b] for b in range(blocks)])
                ch, cl = split(chosen)
                rh, rl = split(right_ref[0, s + i])
                both = mxu(ch, lanes(rh, rl), NN)
                products = both[:, :width] + both[:, width:] + mxu(cl, rh, NN)
                coef = pair_coef(products)
                if i:
                    coef = jnp.where(j >= 0, coef, jnp.zeros_like(coef))
                h, l = split(coef)
                highs.append(h)
                lows.append(l)
            lh0, ll0 = split(left_ref[s])
            lh1, ll1 = split(left_ref[s + 1])
            h, l = lanes(*highs), lanes(*lows)
            lh, ll = lanes(lh0, lh1), lanes(ll0, ll1)
            total = mxu(h, lh, NT_DIMS) + mxu(h, ll, NT_DIMS) + mxu(l, lh, NT_DIMS)
            out_ref[...] -= total.reshape(out_ref.shape)


def gate_tables(count):
    assert 2 * (FIRST_BIN + count - 1) < NT
    cot = lambda m: 1.0 / math.tan(math.pi * m / NT)
    minus = [[0.0 if f == g else cot(g - f) for g in range(count)] for f in range(count)]
    plus = [[cot(f + g + 2 * FIRST_BIN) for g in range(count)] for f in range(count)]
    real = [[0.5 * (minus[f][g] + plus[f][g]) for g in range(count)] for f in range(count)]
    imag = [[0.5 * (plus[f][g] - minus[f][g]) for g in range(count)] for f in range(count)]
    return real, imag


def gate_map(xr, xi, tables):
    real, imag = tables
    count = len(xr)
    total = functools.reduce(lambda a, b: a + b, xr)
    gr, gi = [], []
    for f in range(count):
        a = 0.5 * xr[f] - total
        b = 0.5 * xi[f]
        for g in range(count):
            a = a + real[f][g] * xi[g]
            b = b + imag[f][g] * xr[g]
        gr.append(a)
        gi.append(b)
    return gr, gi


def gate(xr, xi, c1, s1, mark, tables):
    count = len(xr)
    scale = 0.5 / math.sqrt(count * NT)
    ec, es = c1, s1
    power = 1
    while power * 2 <= FIRST_BIN:
        ec, es = ec * ec - es * es, 2.0 * ec * es
        power *= 2
    while power < FIRST_BIN:
        ec, es = ec * c1 - es * s1, ec * s1 + es * c1
        power += 1
    cs, sn = [], []
    for f in range(count):
        cs.append(ec)
        sn.append(es)
        ec, es = ec * c1 - es * s1, ec * s1 + es * c1
    yr = [xr[f] * cs[f] - xi[f] * sn[f] for f in range(count)]
    yi = [xr[f] * sn[f] + xi[f] * cs[f] for f in range(count)]
    hr, hi = gate_map(yr, yi, tables)
    gr, gi = gate_map(xr, xi, tables)
    br = [scale * (cs[f] * hr[f] + sn[f] * hi[f] - gr[f] + mark * xr[f]) for f in range(count)]
    bi = [scale * (cs[f] * hi[f] - sn[f] * hr[f] - gi[f] + mark * xi[f]) for f in range(count)]
    return br, bi


def exchange_kernel(
    nf, ny, chunks, part_ref, trig_ref, out_ref,
    buf1, sums, buf2, xbuf, rbuf, obuf,
    s1s, s1r, s2s, s2r, s3s, s3r, s4s, s4r, s5s, s5r, s6s, s6r,
):
    tables = gate_tables(nf)
    me = lax.axis_index("freq")
    q = lax.axis_index("panel")
    y, c = q // 2, q % 2
    partner = {"panel": y * 2 + 1 - c}
    ypeer = [{"panel": ((y + d) % ny) * 2 + c} for d in range(ny)]
    fpeer = [{"freq": (me + d) % nf} for d in range(nf)]
    MESH = pl.DeviceIdType.MESH

    def send(src, dst, ssem, rsem, device):
        return pltpu.make_async_remote_copy(
            src_ref=src, dst_ref=dst, send_sem=ssem, recv_sem=rsem, device_id=device, device_id_type=MESH
        )

    def block(yy, cc, ch):
        return (yy * 2 + cc) * chunks + ch

    barrier = pltpu.get_barrier_semaphore()
    for dev in [partner] + ypeer[1:] + fpeer[1:]:
        pl.semaphore_signal(barrier, inc=1, device_id=dev, device_id_type=MESH)
    pl.semaphore_wait(barrier, 1 + (ny - 1) + (nf - 1))

    order = list(range(1, ny)) + [0]
    ch_range = range(chunks)
    c1 = [[None] * ny for _ in ch_range]
    for ch in ch_range:
        for d in order:
            c1[ch][d] = send(
                part_ref.at[block((y + d) % ny, 1 - c, ch)], buf1.at[ch, d], s1s.at[ch, d], s1r.at[ch, d], partner
            )
            c1[ch][d].start()

    c2 = [[None] * ny for _ in ch_range]
    c3 = [[None] * nf for _ in ch_range]
    c4 = [[None] * nf for _ in ch_range]
    c5 = [[None] * ny for _ in ch_range]
    c6 = [[None] * ny for _ in ch_range]

    def stage_sum(ch):
        for d in order:
            c1[ch][d].wait_recv()
            sums[ch, d] = part_ref[block((y + d) % ny, c, ch)] + buf1[ch, d]
            if d:
                c2[ch][d] = send(sums.at[ch, d], buf2.at[ch, d - 1], s2s.at[ch, d], s2r.at[ch, d], ypeer[d])
                c2[ch][d].start()

    def stage_out(ch):
        total = sums[ch, 0]
        for d in range(1, ny):
            c2[ch][d].wait_recv()
            total = total + buf2[ch, d - 1]
        xbuf[ch] = total
        for d in range(1, nf):
            to = (me + d) % nf
            c3[ch][d] = send(xbuf.at[ch, :, to], rbuf.at[ch, me], s3s.at[ch, d], s3r.at[ch, d], fpeer[d])
            c3[ch][d].start()
        rbuf[ch, me] = xbuf[ch, :, me]

    def stage_gate(ch):
        for d in range(1, nf):
            c3[ch][d].wait_recv()
        xr = [rbuf[ch, f, 0] for f in range(nf)]
        xi = [rbuf[ch, f, 1] for f in range(nf)]
        br, bi = gate(xr, xi, trig_ref[0, ch], trig_ref[1, ch], trig_ref[2, ch], tables)
        for f in range(nf):
            obuf[ch, f, 0] = br[f]
            obuf[ch, f, 1] = bi[f]
        at = block(y, c, ch)
        for d in range(1, nf):
            to = (me + d) % nf
            c4[ch][d] = send(obuf.at[ch, to], out_ref.at[at, :, me], s4s.at[ch, d], s4r.at[ch, d], fpeer[d])
            c4[ch][d].start()
        out_ref[at, :, me] = obuf[ch, me]

    def stage_back(ch):
        for d in range(1, nf):
            c4[ch][d].wait_recv()
        at = out_ref.at[block(y, c, ch)]
        for d in range(1, ny):
            c5[ch][d] = send(at, at, s5s.at[ch, d], s5r.at[ch, d], ypeer[d])
            c5[ch][d].start()
        c6[ch][0] = send(at, at, s6s.at[ch, 0], s6r.at[ch, 0], partner)
        c6[ch][0].start()

    def stage_pass(ch):
        for d in range(1, ny):
            c5[ch][d].wait_recv()
            at = out_ref.at[block((y + ny - d) % ny, c, ch)]
            c6[ch][d] = send(at, at, s6s.at[ch, d], s6r.at[ch, d], partner)
            c6[ch][d].start()

    stages = [stage_sum, stage_out, stage_gate, stage_back, stage_pass]
    for ch in ch_range:
        stage_sum(ch)
    for step in range(chunks + len(stages) - 2):
        for i, stage in reversed(list(enumerate(stages[1:]))):
            if 0 <= step - i < chunks:
                stage(step - i)
    for ch in ch_range:
        for d in range(ny):
            c6[ch][d].wait_recv()
    for group in (c1, c2, c3, c4, c5, c6):
        for ch in ch_range:
            for copy in group[ch]:
                if copy is not None:
                    copy.wait_send()


def shards(nf, npanel, wavefield, direct, left_factors, right_factors, tile_src, onset):
    panels, slots = tile_src.shape
    rows, width = right_factors.shape[3:]
    virtual = wavefield.shape[2]
    sources = SRC_TILES * rows
    blocks = sources // LANES
    share = sources // npanel
    chunks = share // LANES
    ny = npanel // 2
    vp = virtual // nf
    left = jnp.transpose(left_factors[0], (1, 0, 2))
    right = right_factors[0]
    field = wavefield[0]
    pair = 2 * virtual

    smem = pl.BlockSpec(memory_space=pltpu.SMEM)
    field_spec = pl.BlockSpec((2, virtual, rows), lambda p: (0, 0, p))
    left_spec = pl.BlockSpec((slots, rows, width), lambda p: (0, p, 0))
    right_spec = pl.BlockSpec((1, slots, rows, width), lambda p: (p, 0, 0, 0))
    whole = lambda shape: pl.BlockSpec(shape, lambda p: (0,) * len(shape))

    part, trig = pl.pallas_call(
        functools.partial(adjoint_kernel, share),
        grid=(panels,),
        in_specs=[smem, field_spec, left_spec, right_spec, whole(onset.shape)],
        out_specs=[whole((blocks, pair, LANES)), whole((3, chunks, vp, LANES))],
        out_shape=[
            jax.ShapeDtypeStruct((blocks, pair, LANES), F32),
            jax.ShapeDtypeStruct((3, chunks, vp, LANES), F32),
        ],
        compiler_params=pltpu.CompilerParams(dimension_semantics=("arbitrary",)),
        name="adjoint",
    )(tile_src, field, left, right, onset)

    vmem = pl.BlockSpec(memory_space=pltpu.VMEM)
    dma = lambda n: [pltpu.SemaphoreType.DMA((chunks, n))] * 2
    source = pl.pallas_call(
        functools.partial(exchange_kernel, nf, ny, chunks),
        in_specs=[vmem, vmem],
        out_specs=vmem,
        out_shape=jax.ShapeDtypeStruct((blocks, 2, nf, vp, LANES), F32),
        scratch_shapes=[
            pltpu.VMEM((chunks, ny, 2, nf, vp, LANES), F32),
            pltpu.VMEM((chunks, ny, 2, nf, vp, LANES), F32),
            pltpu.VMEM((chunks, max(ny - 1, 1), 2, nf, vp, LANES), F32),
            pltpu.VMEM((chunks, 2, nf, vp, LANES), F32),
            pltpu.VMEM((chunks, nf, 2, vp, LANES), F32),
            pltpu.VMEM((chunks, nf, 2, vp, LANES), F32),
            *dma(ny), *dma(ny), *dma(nf), *dma(nf), *dma(ny), *dma(ny),
        ],
        compiler_params=pltpu.CompilerParams(collective_id=0, has_side_effects=True),
        name="exchange",
    )(part.reshape(blocks, 2, nf, vp, LANES), trig)

    out = pl.pallas_call(
        forward_kernel,
        grid=(panels,),
        in_specs=[smem, whole((blocks, pair, LANES)), field_spec, left_spec, right_spec],
        out_specs=field_spec,
        out_shape=jax.ShapeDtypeStruct(direct.shape[1:], F32),
        compiler_params=pltpu.CompilerParams(dimension_semantics=("arbitrary",)),
        name="forward",
    )(tile_src, source.reshape(blocks, pair, LANES), direct[0], left, right)
    return out[None]


def solution(mesh):
    in_specs = (
        P("freq", None, None, "panel"),
        P("freq", None, None, "panel"),
        P("freq", "panel", None, None),
        P("freq", "panel", None, None, None),
        P("panel", None),
        P("freq", None),
    )
    out_specs = P("freq", None, None, "panel")
    body = functools.partial(shards, mesh.shape["freq"], mesh.shape["panel"])
    return jax.shard_map(body, mesh=mesh, in_specs=in_specs, out_specs=out_specs, check_vma=False)
```

```python
import functools
import math

import jax
import jax.numpy as jnp
from jax import lax
from jax.experimental import pallas as pl
from jax.experimental.pallas import tpu as pltpu
from jax.sharding import PartitionSpec as P

NT = 1024
FIRST_BIN = 8
SRC_TILES = 8
LANES = 128
BF16 = jnp.bfloat16
F32 = jnp.float32
NN = (((1,), (0,)), ((), ()))
NT_DIMS = (((1,), (1,)), ((), ()))


def split(x):
    high = x.astype(BF16)
    return high, (x - high.astype(F32)).astype(BF16)


def mxu(a, b, dims):
    return lax.dot_general(a, b, dims, preferred_element_type=F32)


def lanes(*parts):
    return jnp.concatenate(parts, axis=1)


def pair_coef(products):
    rows, width = products.shape
    first, second = products[: rows // 2], products[rows // 2 :]
    lane = lax.broadcasted_iota(jnp.int32, first.shape, 1)
    sign = jnp.where(lane < width // 2, 1.0, -1.0).astype(F32)
    swap = lambda x: pltpu.roll(x, width // 2, 1)
    return jnp.concatenate([first + sign * swap(second), second - sign * swap(first)], axis=0)


def adjoint_kernel(share, tile_ref, field_ref, left_ref, right_ref, onset_ref, out_ref, trig_ref):
    p = pl.program_id(0)
    slots, rows, width = left_ref.shape

    @pl.when(p == 0)
    def _():
        out_ref[...] = jnp.zeros_like(out_ref)
        start = lax.axis_index("panel") * share
        for c in range(share // LANES):
            at = pl.multiple_of(start + c * LANES, LANES)
            mark = onset_ref[:, pl.ds(at, LANES)]
            angle = (2.0 * math.pi / NT) * (mark & (NT - 1)).astype(F32)
            trig_ref[0, c] = jnp.cos(angle)
            trig_ref[1, c] = jnp.sin(angle)
            trig_ref[2, c] = mark.astype(F32)

    field = field_ref[...].reshape(-1, rows)
    fh, fl = split(field)
    for s in range(0, slots, 2):

        @pl.when(tile_ref[p, s] >= 0)
        def _(s=s):
            lh0, ll0 = split(left_ref[s])
            lh1, ll1 = split(left_ref[s + 1])
            lh, ll = lanes(lh0, lh1), lanes(ll0, ll1)
            products = mxu(fh, lh, NN) + mxu(fh, ll, NN) + mxu(fl, lh, NN)
            for i in range(2):
                ch, cl = split(pair_coef(products[:, i * width : (i + 1) * width]))
                rh, rl = split(right_ref[0, s + i])
                contrib = mxu(lanes(ch, cl, ch), lanes(rh, rh, rl), NT_DIMS)
                j = tile_ref[p, s + i]

                @pl.when(j >= 0)
                def _(j=j, contrib=contrib):
                    for b in range(rows // LANES):
                        out_ref[j * (rows // LANES) + b] += contrib[:, b * LANES : (b + 1) * LANES]


def forward_kernel(tile_ref, source_ref, direct_ref, left_ref, right_ref, out_ref):
    p = pl.program_id(0)
    slots, rows, width = left_ref.shape
    blocks = rows // LANES
    out_ref[...] = direct_ref[...]
    for s in range(0, slots, 2):

        @pl.when(tile_ref[p, s] >= 0)
        def _(s=s):
            highs, lows = [], []
            for i in range(2):
                j = tile_ref[p, s + i]
                at = jnp.maximum(j, 0)
                chosen = lanes(*[source_ref[at * blocks + b] for b in range(blocks)])
                ch, cl = split(chosen)
                rh, rl = split(right_ref[0, s + i])
                both = mxu(ch, lanes(rh, rl), NN)
                products = both[:, :width] + both[:, width:] + mxu(cl, rh, NN)
                coef = pair_coef(products)
                if i:
                    coef = jnp.where(j >= 0, coef, jnp.zeros_like(coef))
                h, l = split(coef)
                highs.append(h)
                lows.append(l)
            lh0, ll0 = split(left_ref[s])
            lh1, ll1 = split(left_ref[s + 1])
            h, l = lanes(*highs), lanes(*lows)
            lh, ll = lanes(lh0, lh1), lanes(ll0, ll1)
            total = mxu(h, lh, NT_DIMS) + mxu(h, ll, NT_DIMS) + mxu(l, lh, NT_DIMS)
            out_ref[...] -= total.reshape(out_ref.shape)


def gate_tables(count):
    assert 2 * (FIRST_BIN + count - 1) < NT
    cot = lambda m: 1.0 / math.tan(math.pi * m / NT)
    minus = [[0.0 if f == g else cot(g - f) for g in range(count)] for f in range(count)]
    plus = [[cot(f + g + 2 * FIRST_BIN) for g in range(count)] for f in range(count)]
    real = [[0.5 * (minus[f][g] + plus[f][g]) for g in range(count)] for f in range(count)]
    imag = [[0.5 * (plus[f][g] - minus[f][g]) for g in range(count)] for f in range(count)]
    return real, imag


def gate_map(xr, xi, tables):
    real, imag = tables
    count = len(xr)
    total = functools.reduce(lambda a, b: a + b, xr)
    gr, gi = [], []
    for f in range(count):
        a = 0.5 * xr[f] - total
        b = 0.5 * xi[f]
        for g in range(count):
            a = a + real[f][g] * xi[g]
            b = b + imag[f][g] * xr[g]
        gr.append(a)
        gi.append(b)
    return gr, gi


def gate(xr, xi, c1, s1, mark, tables):
    count = len(xr)
    scale = 0.5 / math.sqrt(count * NT)
    ec, es = c1, s1
    power = 1
    while power * 2 <= FIRST_BIN:
        ec, es = ec * ec - es * es, 2.0 * ec * es
        power *= 2
    while power < FIRST_BIN:
        ec, es = ec * c1 - es * s1, ec * s1 + es * c1
        power += 1
    cs, sn = [], []
    for f in range(count):
        cs.append(ec)
        sn.append(es)
        ec, es = ec * c1 - es * s1, ec * s1 + es * c1
    yr = [xr[f] * cs[f] - xi[f] * sn[f] for f in range(count)]
    yi = [xr[f] * sn[f] + xi[f] * cs[f] for f in range(count)]
    hr, hi = gate_map(yr, yi, tables)
    gr, gi = gate_map(xr, xi, tables)
    br = [scale * (cs[f] * hr[f] + sn[f] * hi[f] - gr[f] + mark * xr[f]) for f in range(count)]
    bi = [scale * (cs[f] * hi[f] - sn[f] * hr[f] - gi[f] + mark * xi[f]) for f in range(count)]
    return br, bi


def exchange_kernel(
    nf, ny, chunks, part_ref, trig_ref, out_ref,
    buf1, sums, buf2, xbuf, rbuf, obuf,
    s1s, s1r, s2s, s2r, s3s, s3r, s4s, s4r, s5s, s5r, s6s, s6r,
):
    tables = gate_tables(nf)
    me = lax.axis_index("freq")
    q = lax.axis_index("panel")
    y, c = q // 2, q % 2
    partner = {"panel": y * 2 + 1 - c}
    ypeer = [{"panel": ((y + d) % ny) * 2 + c} for d in range(ny)]
    fpeer = [{"freq": (me + d) % nf} for d in range(nf)]
    MESH = pl.DeviceIdType.MESH

    def send(src, dst, ssem, rsem, device):
        return pltpu.make_async_remote_copy(
            src_ref=src, dst_ref=dst, send_sem=ssem, recv_sem=rsem, device_id=device, device_id_type=MESH
        )

    def block(yy, cc, ch):
        return (yy * 2 + cc) * chunks + ch

    barrier = pltpu.get_barrier_semaphore()
    for dev in [partner] + ypeer[1:] + fpeer[1:]:
        pl.semaphore_signal(barrier, inc=1, device_id=dev, device_id_type=MESH)
    pl.semaphore_wait(barrier, 1 + (ny - 1) + (nf - 1))

    order = list(range(1, ny)) + [0]
    ch_range = range(chunks)
    c1 = [[None] * ny for _ in ch_range]
    for ch in ch_range:
        for d in order:
            c1[ch][d] = send(
                part_ref.at[block((y + d) % ny, 1 - c, ch)], buf1.at[ch, d], s1s.at[ch, d], s1r.at[ch, d], partner
            )
            c1[ch][d].start()

    c2 = [[None] * ny for _ in ch_range]
    c3 = [[None] * nf for _ in ch_range]
    c4 = [[None] * nf for _ in ch_range]
    c5 = [[None] * ny for _ in ch_range]
    c6 = [[None] * ny for _ in ch_range]

    def stage_sum(ch):
        for d in order:
            c1[ch][d].wait_recv()
            sums[ch, d] = part_ref[block((y + d) % ny, c, ch)] + buf1[ch, d]
            if d:
                c2[ch][d] = send(sums.at[ch, d], buf2.at[ch, d - 1], s2s.at[ch, d], s2r.at[ch, d], ypeer[d])
                c2[ch][d].start()

    def stage_out(ch):
        total = sums[ch, 0]
        for d in range(1, ny):
            c2[ch][d].wait_recv()
            total = total + buf2[ch, d - 1]
        xbuf[ch] = total
        for d in range(1, nf):
            to = (me + d) % nf
            c3[ch][d] = send(xbuf.at[ch, :, to], rbuf.at[ch, me], s3s.at[ch, d], s3r.at[ch, d], fpeer[d])
            c3[ch][d].start()
        rbuf[ch, me] = xbuf[ch, :, me]

    def stage_gate(ch):
        for d in range(1, nf):
            c3[ch][d].wait_recv()
        xr = [rbuf[ch, f, 0] for f in range(nf)]
        xi = [rbuf[ch, f, 1] for f in range(nf)]
        br, bi = gate(xr, xi, trig_ref[0, ch], trig_ref[1, ch], trig_ref[2, ch], tables)
        for f in range(nf):
            obuf[ch, f, 0] = br[f]
            obuf[ch, f, 1] = bi[f]
        at = block(y, c, ch)
        for d in range(1, nf):
            to = (me + d) % nf
            c4[ch][d] = send(obuf.at[ch, to], out_ref.at[at, :, me], s4s.at[ch, d], s4r.at[ch, d], fpeer[d])
            c4[ch][d].start()
        out_ref[at, :, me] = obuf[ch, me]

    def stage_back(ch):
        for d in range(1, nf):
            c4[ch][d].wait_recv()
        at = out_ref.at[block(y, c, ch)]
        for d in range(1, ny):
            c5[ch][d] = send(at, at, s5s.at[ch, d], s5r.at[ch, d], ypeer[d])
            c5[ch][d].start()
        c6[ch][0] = send(at, at, s6s.at[ch, 0], s6r.at[ch, 0], partner)
        c6[ch][0].start()

    def stage_pass(ch):
        for d in range(1, ny):
            c5[ch][d].wait_recv()
            at = out_ref.at[block((y + ny - d) % ny, c, ch)]
            c6[ch][d] = send(at, at, s6s.at[ch, d], s6r.at[ch, d], partner)
            c6[ch][d].start()

    stages = [(stage_gate, 2), (stage_out, 0), (stage_back, 3), (stage_pass, 5)]
    for ch in ch_range:
        stage_sum(ch)
    for step in range(chunks + 5):
        for stage, lag in stages:
            if 0 <= step - lag < chunks:
                stage(step - lag)
    for ch in ch_range:
        for d in range(ny):
            c6[ch][d].wait_recv()
    for group in (c1, c2, c3, c4, c5, c6):
        for ch in ch_range:
            for copy in group[ch]:
                if copy is not None:
                    copy.wait_send()


def shards(nf, npanel, wavefield, direct, left_factors, right_factors, tile_src, onset):
    panels, slots = tile_src.shape
    rows, width = right_factors.shape[3:]
    virtual = wavefield.shape[2]
    sources = SRC_TILES * rows
    blocks = sources // LANES
    share = sources // npanel
    chunks = share // LANES
    ny = npanel // 2
    vp = virtual // nf
    left = jnp.transpose(left_factors[0], (1, 0, 2))
    right = right_factors[0]
    field = wavefield[0]
    pair = 2 * virtual

    smem = pl.BlockSpec(memory_space=pltpu.SMEM)
    field_spec = pl.BlockSpec((2, virtual, rows), lambda p: (0, 0, p))
    left_spec = pl.BlockSpec((slots, rows, width), lambda p: (0, p, 0))
    right_spec = pl.BlockSpec((1, slots, rows, width), lambda p: (p, 0, 0, 0))
    whole = lambda shape: pl.BlockSpec(shape, lambda p: (0,) * len(shape))

    part, trig = pl.pallas_call(
        functools.partial(adjoint_kernel, share),
        grid=(panels,),
        in_specs=[smem, field_spec, left_spec, right_spec, whole(onset.shape)],
        out_specs=[whole((blocks, pair, LANES)), whole((3, chunks, vp, LANES))],
        out_shape=[
            jax.ShapeDtypeStruct((blocks, pair, LANES), F32),
            jax.ShapeDtypeStruct((3, chunks, vp, LANES), F32),
        ],
        compiler_params=pltpu.CompilerParams(dimension_semantics=("arbitrary",)),
        name="adjoint",
    )(tile_src, field, left, right, onset)

    vmem = pl.BlockSpec(memory_space=pltpu.VMEM)
    dma = lambda n: [pltpu.SemaphoreType.DMA((chunks, n))] * 2
    source = pl.pallas_call(
        functools.partial(exchange_kernel, nf, ny, chunks),
        in_specs=[vmem, vmem],
        out_specs=vmem,
        out_shape=jax.ShapeDtypeStruct((blocks, 2, nf, vp, LANES), F32),
        scratch_shapes=[
            pltpu.VMEM((chunks, ny, 2, nf, vp, LANES), F32),
            pltpu.VMEM((chunks, ny, 2, nf, vp, LANES), F32),
            pltpu.VMEM((chunks, max(ny - 1, 1), 2, nf, vp, LANES), F32),
            pltpu.VMEM((chunks, 2, nf, vp, LANES), F32),
            pltpu.VMEM((chunks, nf, 2, vp, LANES), F32),
            pltpu.VMEM((chunks, nf, 2, vp, LANES), F32),
            *dma(ny), *dma(ny), *dma(nf), *dma(nf), *dma(ny), *dma(ny),
        ],
        compiler_params=pltpu.CompilerParams(collective_id=0, has_side_effects=True),
        name="exchange",
    )(part.reshape(blocks, 2, nf, vp, LANES), trig)

    out = pl.pallas_call(
        forward_kernel,
        grid=(panels,),
        in_specs=[smem, whole((blocks, pair, LANES)), field_spec, left_spec, right_spec],
        out_specs=field_spec,
        out_shape=jax.ShapeDtypeStruct(direct.shape[1:], F32),
        compiler_params=pltpu.CompilerParams(dimension_semantics=("arbitrary",)),
        name="forward",
    )(tile_src, source.reshape(blocks, pair, LANES), direct[0], left, right)
    return out[None]


def solution(mesh):
    in_specs = (
        P("freq", None, None, "panel"),
        P("freq", None, None, "panel"),
        P("freq", "panel", None, None),
        P("freq", "panel", None, None, None),
        P("panel", None),
        P("freq", None),
    )
    out_specs = P("freq", None, None, "panel")
    body = functools.partial(shards, mesh.shape["freq"], mesh.shape["panel"])
    return jax.shard_map(body, mesh=mesh, in_specs=in_specs, out_specs=out_specs, check_vma=False)
```

```python
import functools
import math

import jax
import jax.numpy as jnp
from jax import lax
from jax.experimental import pallas as pl
from jax.experimental.pallas import tpu as pltpu
from jax.sharding import PartitionSpec as P

NT = 1024
FIRST_BIN = 8
SRC_TILES = 8
LANES = 128
BF16 = jnp.bfloat16
F32 = jnp.float32
NN = (((1,), (0,)), ((), ()))
NT_DIMS = (((1,), (1,)), ((), ()))


def split(x):
    high = x.astype(BF16)
    return high, (x - high.astype(F32)).astype(BF16)


def mxu(a, b, dims):
    return lax.dot_general(a, b, dims, preferred_element_type=F32)


def lanes(*parts):
    return jnp.concatenate(parts, axis=1)


def pair_coef(products):
    rows, width = products.shape
    first, second = products[: rows // 2], products[rows // 2 :]
    lane = lax.broadcasted_iota(jnp.int32, first.shape, 1)
    sign = jnp.where(lane < width // 2, 1.0, -1.0).astype(F32)
    swap = lambda x: pltpu.roll(x, width // 2, 1)
    return jnp.concatenate([first + sign * swap(second), second - sign * swap(first)], axis=0)

def gate_tables(count):
    assert 2 * (FIRST_BIN + count - 1) < NT
    cot = lambda m: 1.0 / math.tan(math.pi * m / NT)
    minus = [[0.0 if f == g else cot(g - f) for g in range(count)] for f in range(count)]
    plus = [[cot(f + g + 2 * FIRST_BIN) for g in range(count)] for f in range(count)]
    real = [[0.5 * (minus[f][g] + plus[f][g]) for g in range(count)] for f in range(count)]
    imag = [[0.5 * (plus[f][g] - minus[f][g]) for g in range(count)] for f in range(count)]
    return real, imag


def gate_map(xr, xi, tables):
    real, imag = tables
    count = len(xr)
    total = functools.reduce(lambda a, b: a + b, xr)
    gr, gi = [], []
    for f in range(count):
        a = 0.5 * xr[f] - total
        b = 0.5 * xi[f]
        for g in range(count):
            a = a + real[f][g] * xi[g]
            b = b + imag[f][g] * xr[g]
        gr.append(a)
        gi.append(b)
    return gr, gi


def gate(xr, xi, c1, s1, mark, tables):
    count = len(xr)
    scale = 0.5 / math.sqrt(count * NT)
    ec, es = c1, s1
    power = 1
    while power * 2 <= FIRST_BIN:
        ec, es = ec * ec - es * es, 2.0 * ec * es
        power *= 2
    while power < FIRST_BIN:
        ec, es = ec * c1 - es * s1, ec * s1 + es * c1
        power += 1
    cs, sn = [], []
    for f in range(count):
        cs.append(ec)
        sn.append(es)
        ec, es = ec * c1 - es * s1, ec * s1 + es * c1
    yr = [xr[f] * cs[f] - xi[f] * sn[f] for f in range(count)]
    yi = [xr[f] * sn[f] + xi[f] * cs[f] for f in range(count)]
    hr, hi = gate_map(yr, yi, tables)
    gr, gi = gate_map(xr, xi, tables)
    br = [scale * (cs[f] * hr[f] + sn[f] * hi[f] - gr[f] + mark * xr[f]) for f in range(count)]
    bi = [scale * (cs[f] * hi[f] - sn[f] * hr[f] - gi[f] + mark * xi[f]) for f in range(count)]
    return br, bi


def unit(mark):
    quarter = NT // 4
    phase = mark & (NT - 1)
    quad = lax.shift_right_logical(phase + quarter // 2, quarter.bit_length() - 1)
    x = (2.0 * math.pi / NT) * (phase - quad * quarter).astype(F32)
    z = x * x
    c = jnp.full_like(x, 1.0 / math.factorial(10))
    s = jnp.full_like(x, 1.0 / math.factorial(11))
    for n in (8, 6, 4, 2, 0):
        c = 1.0 / math.factorial(n) - z * c
    for n in (9, 7, 5, 3, 1):
        s = 1.0 / math.factorial(n) - z * s
    s = s * x
    quad = quad & 3
    swap = (quad & 1) == 1
    cos = jnp.where(swap, s, c)
    sin = jnp.where(swap, c, s)
    cos = jnp.where((quad == 1) | (quad == 2), -cos, cos)
    sin = jnp.where(quad >= 2, -sin, sin)
    return cos, sin


def marchenko_kernel(
    nf, ny, chunks, tile_ref, onset_ref, field_hbm, direct_hbm, left_hbm, right_hbm, out_hbm,
    field, direct, left, right, coef_h, coef_l, left_h, left_l, right_h, right_l,
    part, buf1, sums, buf2, xbuf, rbuf, obuf, source, chosen_ref,
    field_sem, direct_sem, left_sem, right_sem, out_sem,
    s1s, s1r, s2s, s2r, s3s, s3r, s4s, s4r, s5s, s5r, s6s, s6r,
):
    tables = gate_tables(nf)
    panels, slots, rows, width = right.shape
    pair = part.shape[1]
    virtual = pair // 2
    vp = virtual // nf
    blocks = rows // LANES
    np_ = 2 * ny
    tiles = np_ // blocks
    me = lax.axis_index("freq")
    q = lax.axis_index("panel")
    y, c = q // 2, q % 2
    partner = {"panel": y * 2 + 1 - c}
    ypeer = [{"panel": ((y + d) % ny) * 2 + c} for d in range(ny)]
    fpeer = [{"freq": (me + d) % nf} for d in range(nf)]
    MESH = pl.DeviceIdType.MESH

    loads_a, loads_b, loads_c = [], [], []
    for p in range(panels):
        cols = pl.ds(p * rows, rows)
        loads_a.append(pltpu.make_async_copy(field_hbm.at[:, :, cols], field.at[p], field_sem.at[p]))
        loads_a.append(pltpu.make_async_copy(left_hbm.at[:, cols, :], left.at[p], left_sem.at[p]))
        loads_b.append(pltpu.make_async_copy(right_hbm.at[p], right.at[p], right_sem.at[p]))
        loads_c.append(pltpu.make_async_copy(direct_hbm.at[:, :, cols], direct.at[p], direct_sem.at[p]))
    for copy in loads_a + loads_b + loads_c:
        copy.start()

    barrier = pltpu.get_barrier_semaphore()
    for dev in [partner] + ypeer[1:] + fpeer[1:]:
        pl.semaphore_signal(barrier, inc=1, device_id=dev, device_id_type=MESH)

    def slot_of(p, j):
        slot = jnp.int32(slots)
        for s in range(slots):
            slot = jnp.where(tile_ref[p, s] == j, jnp.int32(s), slot)
        return slot

    zero = jnp.zeros((pair, width), BF16)
    for p in range(panels):
        coef_h[p, slots] = zero
        coef_l[p, slots] = zero
        left_h[p, slots] = zero[:rows]
        left_l[p, slots] = zero[:rows]

    for p in range(panels):
        loads_a[2 * p].wait()
        loads_a[2 * p + 1].wait()
        fh, fl = split(field[p].reshape(pair, rows))
        fcat = lanes(fh, fh, fl)
        for s in range(0, slots, 2):
            halves = []
            for i in range(2):
                h, l = split(left[p, s + i])
                left_h[p, s + i] = h
                left_l[p, s + i] = l
                halves.append(jnp.concatenate([h, l, h], axis=0))
            products = mxu(fcat, lanes(*halves), NN)
            for i in range(2):
                h, l = split(pair_coef(products[:, i * width : (i + 1) * width]))
                coef_h[p, s + i] = h
                coef_l[p, s + i] = l
    for p in range(panels):
        loads_b[p].wait()
        for s in range(slots):
            h, l = split(right[p, s])
            right_h[p, s] = h
            right_l[p, s] = l

    def send(src, dst, ssem, rsem, device):
        copy = pltpu.make_async_remote_copy(
            src_ref=src, dst_ref=dst, send_sem=ssem, recv_sem=rsem, device_id=device, device_id_type=MESH
        )
        copy.start()
        return copy

    def block(yy, cc, ch):
        return ch * np_ + yy * 2 + cc

    order = list(range(1, ny)) + [0]
    c1 = [[None] * ny for _ in range(chunks)]
    c2 = [[None] * ny for _ in range(chunks)]
    c3 = [[None] * nf for _ in range(chunks)]
    c4 = [[None] * nf for _ in range(chunks)]
    c5 = [[None] * ny for _ in range(chunks)]
    c6 = [[None] * ny for _ in range(chunks)]

    def stage_adjoint(ch):
        for j in range(ch * tiles, (ch + 1) * tiles):
            ins, outs = [], []
            for p in range(panels):
                slot = slot_of(p, j)
                real = jnp.minimum(slot, slots - 1)
                h, l = coef_h[p, slot], coef_l[p, slot]
                rh, rl = right_h[p, real], right_l[p, real]
                ins += [h, l, h]
                outs += [rh, rh, rl]
            tile = mxu(lanes(*ins), lanes(*outs), NT_DIMS)
            for b in range(blocks):
                part[j * blocks + b] = tile[:, b * LANES : (b + 1) * LANES]
        if ch == 0:
            pl.semaphore_wait(barrier, 1 + (ny - 1) + (nf - 1))
        for d in order:
            c1[ch][d] = send(
                part.at[block((y + d) % ny, 1 - c, ch)], buf1.at[ch, d], s1s.at[ch, d], s1r.at[ch, d], partner
            )

    def stage_sum(ch):
        for d in order:
            c1[ch][d].wait_recv()
            sums[ch, d] = part[block((y + d) % ny, c, ch)] + buf1[ch, d]
            if d:
                c2[ch][d] = send(sums.at[ch, d], buf2.at[ch, d - 1], s2s.at[ch, d], s2r.at[ch, d], ypeer[d])

    def stage_out(ch):
        total = sums[ch, 0]
        for d in range(1, ny):
            c2[ch][d].wait_recv()
            total = total + buf2[ch, d - 1]
        if vp % 8 == 0:
            xbuf[ch] = total.reshape(2, nf, vp, LANES)
        else:
            for k in range(2 * nf):
                xbuf[ch, k // nf, k % nf] = total[k * vp : (k + 1) * vp]
        for d in range(1, nf):
            to = (me + d) % nf
            c3[ch][d] = send(xbuf.at[ch, :, to], rbuf.at[ch, me], s3s.at[ch, d], s3r.at[ch, d], fpeer[d])
        rbuf[ch, me] = xbuf[ch, :, me]

    def stage_gate(ch):
        at = block(y, c, ch)
        mark = onset_ref[:, pl.ds(pl.multiple_of(at * LANES, LANES), LANES)]
        cos, sin = unit(mark)
        for d in range(1, nf):
            c3[ch][d].wait_recv()
        xr = [rbuf[ch, f, 0] for f in range(nf)]
        xi = [rbuf[ch, f, 1] for f in range(nf)]
        br, bi = gate(xr, xi, cos, sin, mark.astype(F32), tables)
        for f in range(nf):
            obuf[ch, f, 0] = br[f]
            obuf[ch, f, 1] = bi[f]
        for d in range(1, nf):
            to = (me + d) % nf
            c4[ch][d] = send(obuf.at[ch, to], source.at[at, :, me], s4s.at[ch, d], s4r.at[ch, d], fpeer[d])
        source[at, :, me] = obuf[ch, me]

    def stage_back(ch):
        for d in range(1, nf):
            c4[ch][d].wait_recv()
        at = source.at[block(y, c, ch)]
        for d in range(1, ny):
            c5[ch][d] = send(at, at, s5s.at[ch, d], s5r.at[ch, d], ypeer[d])
        c6[ch][0] = send(at, at, s6s.at[ch, 0], s6r.at[ch, 0], partner)

    def stage_pass(ch):
        for d in range(1, ny):
            c5[ch][d].wait_recv()
            at = source.at[block((y + ny - d) % ny, c, ch)]
            c6[ch][d] = send(at, at, s6s.at[ch, d], s6r.at[ch, d], partner)

    def load_block(b):
        if vp % 8 == 0:
            return source[b].reshape(pair, LANES)
        for k in range(2 * nf):
            chosen_ref[k * vp : (k + 1) * vp, :] = source[b, k // nf, k % nf]
        return chosen_ref[...]

    stores = []

    def stage_forward(ch):
        for d in range(ny):
            c6[ch][d].wait_recv()
        left_in = [[] for _ in range(panels)]
        left_w = [[] for _ in range(panels)]
        for j in range(ch * tiles, (ch + 1) * tiles):
            h, l = split(lanes(*[load_block(j * blocks + b) for b in range(blocks)]))
            at = [slot_of(p, j) for p in range(panels)]
            real = [jnp.minimum(a, slots - 1) for a in at]
            rh = lanes(*[right_h[p, real[p]] for p in range(panels)])
            rl = lanes(*[right_l[p, real[p]] for p in range(panels)])
            products = mxu(lanes(h, h, l), jnp.concatenate([rh, rl, rh], axis=0), NN)
            for p in range(panels):
                ph, plow = split(pair_coef(products[:, p * width : (p + 1) * width]))
                lh, ll = left_h[p, at[p]], left_l[p, at[p]]
                left_in[p] += [ph, ph, plow]
                left_w[p] += [lh, ll, lh]
        for p in range(panels):
            if ch == 0:
                loads_c[p].wait()
            total = mxu(lanes(*left_in[p]), lanes(*left_w[p]), NT_DIMS)
            direct[p] -= total.reshape(2, virtual, rows)
            if ch == chunks - 1:
                store = pltpu.make_async_copy(
                    direct.at[p], out_hbm.at[:, :, pl.ds(p * rows, rows)], out_sem.at[p]
                )
                store.start()
                stores.append(store)

    for ch in range(chunks):
        stage_adjoint(ch)
        if ch:
            stage_sum(ch - 1)
    stage_sum(chunks - 1)
    stages = [(stage_gate, 2), (stage_out, 0), (stage_back, 3), (stage_pass, 5), (stage_forward, 6)]
    for step in range(chunks + 6):
        for stage, lag in stages:
            if 0 <= step - lag < chunks:
                stage(step - lag)
    for group in (c1, c2, c3, c4, c5, c6):
        for ch in range(chunks):
            for copy in group[ch]:
                if copy is not None:
                    copy.wait_send()
    for store in stores:
        store.wait()


def shards(nf, npanel, wavefield, direct, left_factors, right_factors, tile_src, onset):
    panels, slots = tile_src.shape
    rows, width = right_factors.shape[3:]
    virtual = wavefield.shape[2]
    blocks = SRC_TILES * rows // LANES
    chunks = blocks // npanel
    ny = npanel // 2
    vp = virtual // nf
    pair = 2 * virtual
    left = jnp.transpose(left_factors[0], (1, 0, 2))
    hbm = pl.BlockSpec(memory_space=pl.ANY)
    dma = lambda n: [pltpu.SemaphoreType.DMA((chunks, n))] * 2
    split_buf = lambda n, r: [pltpu.VMEM((panels, n, r, width), BF16)] * 2
    out = pl.pallas_call(
        functools.partial(marchenko_kernel, nf, ny, chunks),
        in_specs=[
            pl.BlockSpec(memory_space=pltpu.SMEM), pl.BlockSpec(memory_space=pltpu.VMEM), hbm, hbm, hbm, hbm,
        ],
        out_specs=hbm,
        out_shape=jax.ShapeDtypeStruct(direct.shape[1:], F32),
        scratch_shapes=[
            pltpu.VMEM((panels, 2, virtual, rows), F32),
            pltpu.VMEM((panels, 2, virtual, rows), F32),
            pltpu.VMEM((panels, slots, rows, width), F32),
            pltpu.VMEM((panels, slots, rows, width), F32),
            *split_buf(slots + 1, pair),
            *split_buf(slots + 1, rows),
            *split_buf(slots, rows),
            pltpu.VMEM((blocks, pair, LANES), F32),
            pltpu.VMEM((chunks, ny, pair, LANES), F32),
            pltpu.VMEM((chunks, ny, pair, LANES), F32),
            pltpu.VMEM((chunks, ny - 1, pair, LANES), F32),
            pltpu.VMEM((chunks, 2, nf, vp, LANES), F32),
            pltpu.VMEM((chunks, nf, 2, vp, LANES), F32),
            pltpu.VMEM((chunks, nf, 2, vp, LANES), F32),
            pltpu.VMEM((blocks, 2, nf, vp, LANES), F32),
            pltpu.VMEM((pair, LANES), F32),
            *[pltpu.SemaphoreType.DMA((panels,))] * 5,
            *dma(ny), *dma(ny), *dma(nf), *dma(nf), *dma(ny), *dma(ny),
        ],
        compiler_params=pltpu.CompilerParams(collective_id=0, has_side_effects=True),
        name="marchenko",
    )(tile_src, onset, wavefield[0], direct[0], left, right_factors[0])
    return out[None]


def solution(mesh):
    in_specs = (
        P("freq", None, None, "panel"),
        P("freq", None, None, "panel"),
        P("freq", "panel", None, None),
        P("freq", "panel", None, None, None),
        P("panel", None),
        P("freq", None),
    )
    out_specs = P("freq", None, None, "panel")
    body = functools.partial(shards, mesh.shape["freq"], mesh.shape["panel"])
    return jax.shard_map(body, mesh=mesh, in_specs=in_specs, out_specs=out_specs, check_vma=False)
```

```python
import functools
import math

import jax
import jax.numpy as jnp
from jax import lax
from jax.experimental import pallas as pl
from jax.experimental.pallas import tpu as pltpu
from jax.sharding import PartitionSpec as P

NT = 1024
FIRST_BIN = 8
SRC_TILES = 8
LANES = 128
BF16 = jnp.bfloat16
F32 = jnp.float32
NN = (((1,), (0,)), ((), ()))
NT_DIMS = (((1,), (1,)), ((), ()))


def split(x):
    high = x.astype(BF16)
    return high, (x - high.astype(F32)).astype(BF16)


def mxu(a, b, dims):
    return lax.dot_general(a, b, dims, preferred_element_type=F32)


def lanes(*parts):
    return jnp.concatenate(parts, axis=1)


def pair_coef(products):
    rows, width = products.shape
    first, second = products[: rows // 2], products[rows // 2 :]
    lane = lax.broadcasted_iota(jnp.int32, first.shape, 1)
    sign = jnp.where(lane < width // 2, 1.0, -1.0).astype(F32)
    swap = lambda x: pltpu.roll(x, width // 2, 1)
    return jnp.concatenate([first + sign * swap(second), second - sign * swap(first)], axis=0)

def gate_tables(count):
    assert 2 * (FIRST_BIN + count - 1) < NT
    cot = lambda m: 1.0 / math.tan(math.pi * m / NT)
    minus = [[0.0 if f == g else cot(g - f) for g in range(count)] for f in range(count)]
    plus = [[cot(f + g + 2 * FIRST_BIN) for g in range(count)] for f in range(count)]
    real = [[0.5 * (minus[f][g] + plus[f][g]) for g in range(count)] for f in range(count)]
    imag = [[0.5 * (plus[f][g] - minus[f][g]) for g in range(count)] for f in range(count)]
    return real, imag


def gate_map(xr, xi, tables):
    real, imag = tables
    count = len(xr)
    total = functools.reduce(lambda a, b: a + b, xr)
    gr, gi = [], []
    for f in range(count):
        a = 0.5 * xr[f] - total
        b = 0.5 * xi[f]
        for g in range(count):
            a = a + real[f][g] * xi[g]
            b = b + imag[f][g] * xr[g]
        gr.append(a)
        gi.append(b)
    return gr, gi


def gate(xr, xi, c1, s1, mark, tables):
    count = len(xr)
    scale = 0.5 / math.sqrt(count * NT)
    ec, es = c1, s1
    power = 1
    while power * 2 <= FIRST_BIN:
        ec, es = ec * ec - es * es, 2.0 * ec * es
        power *= 2
    while power < FIRST_BIN:
        ec, es = ec * c1 - es * s1, ec * s1 + es * c1
        power += 1
    cs, sn = [], []
    for f in range(count):
        cs.append(ec)
        sn.append(es)
        ec, es = ec * c1 - es * s1, ec * s1 + es * c1
    yr = [xr[f] * cs[f] - xi[f] * sn[f] for f in range(count)]
    yi = [xr[f] * sn[f] + xi[f] * cs[f] for f in range(count)]
    hr, hi = gate_map(yr, yi, tables)
    gr, gi = gate_map(xr, xi, tables)
    br = [scale * (cs[f] * hr[f] + sn[f] * hi[f] - gr[f] + mark * xr[f]) for f in range(count)]
    bi = [scale * (cs[f] * hi[f] - sn[f] * hr[f] - gi[f] + mark * xi[f]) for f in range(count)]
    return br, bi


def unit(mark):
    quarter = NT // 4
    phase = mark & (NT - 1)
    quad = lax.shift_right_logical(phase + quarter // 2, quarter.bit_length() - 1)
    x = (2.0 * math.pi / NT) * (phase - quad * quarter).astype(F32)
    z = x * x
    c = jnp.full_like(x, 1.0 / math.factorial(10))
    s = jnp.full_like(x, 1.0 / math.factorial(11))
    for n in (8, 6, 4, 2, 0):
        c = 1.0 / math.factorial(n) - z * c
    for n in (9, 7, 5, 3, 1):
        s = 1.0 / math.factorial(n) - z * s
    s = s * x
    quad = quad & 3
    swap = (quad & 1) == 1
    cos = jnp.where(swap, s, c)
    sin = jnp.where(swap, c, s)
    cos = jnp.where((quad == 1) | (quad == 2), -cos, cos)
    sin = jnp.where(quad >= 2, -sin, sin)
    return cos, sin


def marchenko_kernel(
    nf, ny, chunks, tile_ref, onset_ref, field_hbm, direct_hbm, left_hbm, right_hbm, out_ref,
    field, direct, left, right, coef_h, coef_l, left_h, left_l, right_h, right_l,
    part, buf1, sums, buf2, xbuf, rbuf, obuf, source, chosen_ref,
    field_sem, direct_sem, left_sem, right_sem,
    s1s, s1r, s2s, s2r, s3s, s3r, s4s, s4r, s5s, s5r, s6s, s6r,
):
    tables = gate_tables(nf)
    panels, slots, rows, width = right.shape
    pair = part.shape[1]
    virtual = pair // 2
    vp = virtual // nf
    blocks = rows // LANES
    np_ = 2 * ny
    tiles = np_ // blocks
    me = lax.axis_index("freq")
    q = lax.axis_index("panel")
    y, c = q // 2, q % 2
    partner = {"panel": y * 2 + 1 - c}
    ypeer = [{"panel": ((y + d) % ny) * 2 + c} for d in range(ny)]
    fpeer = [{"freq": (me + d) % nf} for d in range(nf)]
    MESH = pl.DeviceIdType.MESH

    loads_a, loads_b, loads_c = [], [], []
    for p in range(panels):
        cols = pl.ds(p * rows, rows)
        loads_a.append(pltpu.make_async_copy(field_hbm.at[:, :, cols], field.at[p], field_sem.at[p]))
        loads_a.append(pltpu.make_async_copy(left_hbm.at[:, cols, :], left.at[p], left_sem.at[p]))
        loads_b.append(pltpu.make_async_copy(right_hbm.at[p], right.at[p], right_sem.at[p]))
        loads_c.append(pltpu.make_async_copy(direct_hbm.at[:, :, cols], direct.at[p], direct_sem.at[p]))
    for copy in loads_a + loads_b + loads_c:
        copy.start()

    barrier = pltpu.get_barrier_semaphore()
    for dev in [partner] + ypeer[1:] + fpeer[1:]:
        pl.semaphore_signal(barrier, inc=1, device_id=dev, device_id_type=MESH)

    def slot_of(p, j):
        slot = jnp.int32(slots)
        for s in range(slots):
            slot = jnp.where(tile_ref[p, s] == j, jnp.int32(s), slot)
        return slot

    zero = jnp.zeros((pair, width), BF16)
    for p in range(panels):
        coef_h[p, slots] = zero
        coef_l[p, slots] = zero
        left_h[p, slots] = zero[:rows]
        left_l[p, slots] = zero[:rows]

    for p in range(panels):
        loads_a[2 * p].wait()
        loads_a[2 * p + 1].wait()
        fh, fl = split(field[p].reshape(pair, rows))
        fcat = lanes(fh, fh, fl)
        for s in range(0, slots, 2):
            halves = []
            for i in range(2):
                h, l = split(left[p, s + i])
                left_h[p, s + i] = h
                left_l[p, s + i] = l
                halves.append(jnp.concatenate([h, l, h], axis=0))
            products = mxu(fcat, lanes(*halves), NN)
            for i in range(2):
                h, l = split(pair_coef(products[:, i * width : (i + 1) * width]))
                coef_h[p, s + i] = h
                coef_l[p, s + i] = l
    for p in range(panels):
        loads_b[p].wait()
        for s in range(slots):
            h, l = split(right[p, s])
            right_h[p, s] = h
            right_l[p, s] = l

    def send(src, dst, ssem, rsem, device):
        copy = pltpu.make_async_remote_copy(
            src_ref=src, dst_ref=dst, send_sem=ssem, recv_sem=rsem, device_id=device, device_id_type=MESH
        )
        copy.start()
        return copy

    def block(yy, cc, ch):
        return ch * np_ + yy * 2 + cc

    order = list(range(1, ny)) + [0]
    c1 = [[None] * ny for _ in range(chunks)]
    c2 = [[None] * ny for _ in range(chunks)]
    c3 = [[None] * nf for _ in range(chunks)]
    c4 = [[None] * nf for _ in range(chunks)]
    c5 = [[None] * ny for _ in range(chunks)]
    c6 = [[None] * ny for _ in range(chunks)]

    def stage_adjoint(ch):
        for j in range(ch * tiles, (ch + 1) * tiles):
            ins, outs = [], []
            for p in range(panels):
                slot = slot_of(p, j)
                real = jnp.minimum(slot, slots - 1)
                h, l = coef_h[p, slot], coef_l[p, slot]
                rh, rl = right_h[p, real], right_l[p, real]
                ins += [h, l, h]
                outs += [rh, rh, rl]
            tile = mxu(lanes(*ins), lanes(*outs), NT_DIMS)
            for b in range(blocks):
                part[j * blocks + b] = tile[:, b * LANES : (b + 1) * LANES]
        if ch == 0:
            pl.semaphore_wait(barrier, 1 + (ny - 1) + (nf - 1))
        for d in order:
            c1[ch][d] = send(
                part.at[block((y + d) % ny, 1 - c, ch)], buf1.at[ch, d], s1s.at[ch, d], s1r.at[ch, d], partner
            )

    def stage_sum(ch):
        for d in order:
            c1[ch][d].wait_recv()
            sums[ch, d] = part[block((y + d) % ny, c, ch)] + buf1[ch, d]
            if d:
                c2[ch][d] = send(sums.at[ch, d], buf2.at[ch, d - 1], s2s.at[ch, d], s2r.at[ch, d], ypeer[d])

    def stage_out(ch):
        total = sums[ch, 0]
        for d in range(1, ny):
            c2[ch][d].wait_recv()
            total = total + buf2[ch, d - 1]
        if vp % 8 == 0:
            xbuf[ch] = total.reshape(2, nf, vp, LANES)
        else:
            for k in range(2 * nf):
                xbuf[ch, k // nf, k % nf] = total[k * vp : (k + 1) * vp]
        for d in range(1, nf):
            to = (me + d) % nf
            c3[ch][d] = send(xbuf.at[ch, :, to], rbuf.at[ch, me], s3s.at[ch, d], s3r.at[ch, d], fpeer[d])
        rbuf[ch, me] = xbuf[ch, :, me]

    def stage_gate(ch):
        at = block(y, c, ch)
        mark = onset_ref[:, pl.ds(pl.multiple_of(at * LANES, LANES), LANES)]
        cos, sin = unit(mark)
        for d in range(1, nf):
            c3[ch][d].wait_recv()
        xr = [rbuf[ch, f, 0] for f in range(nf)]
        xi = [rbuf[ch, f, 1] for f in range(nf)]
        br, bi = gate(xr, xi, cos, sin, mark.astype(F32), tables)
        for f in range(nf):
            obuf[ch, f, 0] = br[f]
            obuf[ch, f, 1] = bi[f]
        for d in range(1, nf):
            to = (me + d) % nf
            c4[ch][d] = send(obuf.at[ch, to], source.at[at, :, me], s4s.at[ch, d], s4r.at[ch, d], fpeer[d])
        source[at, :, me] = obuf[ch, me]

    def stage_back(ch):
        for d in range(1, nf):
            c4[ch][d].wait_recv()
        at = source.at[block(y, c, ch)]
        for d in range(1, ny):
            c5[ch][d] = send(at, at, s5s.at[ch, d], s5r.at[ch, d], ypeer[d])
        c6[ch][0] = send(at, at, s6s.at[ch, 0], s6r.at[ch, 0], partner)

    def stage_pass(ch):
        for d in range(1, ny):
            c5[ch][d].wait_recv()
            at = source.at[block((y + ny - d) % ny, c, ch)]
            c6[ch][d] = send(at, at, s6s.at[ch, d], s6r.at[ch, d], partner)

    def load_block(b):
        if vp % 8 == 0:
            return source[b].reshape(pair, LANES)
        for k in range(2 * nf):
            chosen_ref[k * vp : (k + 1) * vp, :] = source[b, k // nf, k % nf]
        return chosen_ref[...]

    def stage_forward(ch):
        for d in range(ny):
            c6[ch][d].wait_recv()
        left_in = [[] for _ in range(panels)]
        left_w = [[] for _ in range(panels)]
        for j in range(ch * tiles, (ch + 1) * tiles):
            h, l = split(lanes(*[load_block(j * blocks + b) for b in range(blocks)]))
            at = [slot_of(p, j) for p in range(panels)]
            real = [jnp.minimum(a, slots - 1) for a in at]
            rh = lanes(*[right_h[p, real[p]] for p in range(panels)])
            rl = lanes(*[right_l[p, real[p]] for p in range(panels)])
            products = mxu(lanes(h, h, l), jnp.concatenate([rh, rl, rh], axis=0), NN)
            for p in range(panels):
                ph, plow = split(pair_coef(products[:, p * width : (p + 1) * width]))
                lh, ll = left_h[p, at[p]], left_l[p, at[p]]
                left_in[p] += [ph, ph, plow]
                left_w[p] += [lh, ll, lh]
        for p in range(panels):
            if ch == 0:
                loads_c[p].wait()
            total = mxu(lanes(*left_in[p]), lanes(*left_w[p]), NT_DIMS)
            done = direct[p] - total.reshape(2, virtual, rows)
            if ch == chunks - 1:
                out_ref[:, :, p * rows : (p + 1) * rows] = done
            else:
                direct[p] = done

    for ch in range(chunks):
        stage_adjoint(ch)
        if ch:
            stage_sum(ch - 1)
    stage_sum(chunks - 1)
    stages = [(stage_gate, 2), (stage_out, 0), (stage_back, 3), (stage_pass, 5), (stage_forward, 6)]
    for step in range(chunks + 6):
        for stage, lag in stages:
            if 0 <= step - lag < chunks:
                stage(step - lag)
    for group in (c1, c2, c3, c4, c5, c6):
        for ch in range(chunks):
            for copy in group[ch]:
                if copy is not None:
                    copy.wait_send()


def shards(nf, npanel, wavefield, direct, left_factors, right_factors, tile_src, onset):
    panels, slots = tile_src.shape
    rows, width = right_factors.shape[3:]
    virtual = wavefield.shape[2]
    blocks = SRC_TILES * rows // LANES
    chunks = blocks // npanel
    ny = npanel // 2
    vp = virtual // nf
    pair = 2 * virtual
    left = jnp.transpose(left_factors[0], (1, 0, 2))
    hbm = pl.BlockSpec(memory_space=pl.ANY)
    dma = lambda n: [pltpu.SemaphoreType.DMA((chunks, n))] * 2
    split_buf = lambda n, r: [pltpu.VMEM((panels, n, r, width), BF16)] * 2
    out = pl.pallas_call(
        functools.partial(marchenko_kernel, nf, ny, chunks),
        in_specs=[
            pl.BlockSpec(memory_space=pltpu.SMEM), pl.BlockSpec(memory_space=pltpu.VMEM), hbm, hbm, hbm, hbm,
        ],
        out_specs=pl.BlockSpec(memory_space=pltpu.VMEM),
        out_shape=pltpu.VMEM(direct.shape[1:], F32),
        scratch_shapes=[
            pltpu.VMEM((panels, 2, virtual, rows), F32),
            pltpu.VMEM((panels, 2, virtual, rows), F32),
            pltpu.VMEM((panels, slots, rows, width), F32),
            pltpu.VMEM((panels, slots, rows, width), F32),
            *split_buf(slots + 1, pair),
            *split_buf(slots + 1, rows),
            *split_buf(slots, rows),
            pltpu.VMEM((blocks, pair, LANES), F32),
            pltpu.VMEM((chunks, ny, pair, LANES), F32),
            pltpu.VMEM((chunks, ny, pair, LANES), F32),
            pltpu.VMEM((chunks, ny - 1, pair, LANES), F32),
            pltpu.VMEM((chunks, 2, nf, vp, LANES), F32),
            pltpu.VMEM((chunks, nf, 2, vp, LANES), F32),
            pltpu.VMEM((chunks, nf, 2, vp, LANES), F32),
            pltpu.VMEM((blocks, 2, nf, vp, LANES), F32),
            pltpu.VMEM((pair, LANES), F32),
            *[pltpu.SemaphoreType.DMA((panels,))] * 4,
            *dma(ny), *dma(ny), *dma(nf), *dma(nf), *dma(ny), *dma(ny),
        ],
        compiler_params=pltpu.CompilerParams(collective_id=0, has_side_effects=True),
        name="marchenko",
    )(tile_src, onset, wavefield[0], direct[0], left, right_factors[0])
    return out[None]


def solution(mesh):
    in_specs = (
        P("freq", None, None, "panel"),
        P("freq", None, None, "panel"),
        P("freq", "panel", None, None),
        P("freq", "panel", None, None, None),
        P("panel", None),
        P("freq", None),
    )
    out_specs = P("freq", None, None, "panel")
    body = functools.partial(shards, mesh.shape["freq"], mesh.shape["panel"])
    return jax.shard_map(body, mesh=mesh, in_specs=in_specs, out_specs=out_specs, check_vma=False)
```

```python
import functools
import math

import jax
import jax.numpy as jnp
from jax import lax
from jax.experimental import pallas as pl
from jax.experimental.pallas import tpu as pltpu
from jax.sharding import PartitionSpec as P

NT = 1024
FIRST_BIN = 8
SRC_TILES = 8
LANES = 128
BF16 = jnp.bfloat16
F32 = jnp.float32
NN = (((1,), (0,)), ((), ()))
NT_DIMS = (((1,), (1,)), ((), ()))


def split(x):
    high = x.astype(BF16)
    return high, (x - high.astype(F32)).astype(BF16)


def mxu(a, b, dims):
    return lax.dot_general(a, b, dims, preferred_element_type=F32)


def lanes(*parts):
    return jnp.concatenate(parts, axis=1)


def pair_coef(products):
    rows, width = products.shape
    first, second = products[: rows // 2], products[rows // 2 :]
    lane = lax.broadcasted_iota(jnp.int32, first.shape, 1)
    sign = jnp.where(lane < width // 2, 1.0, -1.0).astype(F32)
    swap = lambda x: pltpu.roll(x, width // 2, 1)
    return jnp.concatenate([first + sign * swap(second), second - sign * swap(first)], axis=0)

def gate_tables(count):
    assert 2 * (FIRST_BIN + count - 1) < NT
    cot = lambda m: 1.0 / math.tan(math.pi * m / NT)
    minus = [[0.0 if f == g else cot(g - f) for g in range(count)] for f in range(count)]
    plus = [[cot(f + g + 2 * FIRST_BIN) for g in range(count)] for f in range(count)]
    real = [[0.5 * (minus[f][g] + plus[f][g]) for g in range(count)] for f in range(count)]
    imag = [[0.5 * (plus[f][g] - minus[f][g]) for g in range(count)] for f in range(count)]
    return real, imag


def gate_map(xr, xi, tables):
    real, imag = tables
    count = len(xr)
    total = functools.reduce(lambda a, b: a + b, xr)
    gr, gi = [], []
    for f in range(count):
        a = 0.5 * xr[f] - total
        b = 0.5 * xi[f]
        for g in range(count):
            a = a + real[f][g] * xi[g]
            b = b + imag[f][g] * xr[g]
        gr.append(a)
        gi.append(b)
    return gr, gi


def gate(xr, xi, c1, s1, mark, tables):
    count = len(xr)
    scale = 0.5 / math.sqrt(count * NT)
    ec, es = c1, s1
    power = 1
    while power * 2 <= FIRST_BIN:
        ec, es = ec * ec - es * es, 2.0 * ec * es
        power *= 2
    while power < FIRST_BIN:
        ec, es = ec * c1 - es * s1, ec * s1 + es * c1
        power += 1
    cs, sn = [], []
    for f in range(count):
        cs.append(ec)
        sn.append(es)
        ec, es = ec * c1 - es * s1, ec * s1 + es * c1
    yr = [xr[f] * cs[f] - xi[f] * sn[f] for f in range(count)]
    yi = [xr[f] * sn[f] + xi[f] * cs[f] for f in range(count)]
    hr, hi = gate_map(yr, yi, tables)
    gr, gi = gate_map(xr, xi, tables)
    br = [scale * (cs[f] * hr[f] + sn[f] * hi[f] - gr[f] + mark * xr[f]) for f in range(count)]
    bi = [scale * (cs[f] * hi[f] - sn[f] * hr[f] - gi[f] + mark * xi[f]) for f in range(count)]
    return br, bi


def unit(mark):
    quarter = NT // 4
    phase = mark & (NT - 1)
    quad = lax.shift_right_logical(phase + quarter // 2, quarter.bit_length() - 1)
    x = (2.0 * math.pi / NT) * (phase - quad * quarter).astype(F32)
    z = x * x
    c = jnp.full_like(x, 1.0 / math.factorial(10))
    s = jnp.full_like(x, 1.0 / math.factorial(11))
    for n in (8, 6, 4, 2, 0):
        c = 1.0 / math.factorial(n) - z * c
    for n in (9, 7, 5, 3, 1):
        s = 1.0 / math.factorial(n) - z * s
    s = s * x
    quad = quad & 3
    swap = (quad & 1) == 1
    cos = jnp.where(swap, s, c)
    sin = jnp.where(swap, c, s)
    cos = jnp.where((quad == 1) | (quad == 2), -cos, cos)
    sin = jnp.where(quad >= 2, -sin, sin)
    return cos, sin


def marchenko_kernel(
    nf, ny, chunks, tile_ref, onset_ref, field_hbm, direct_hbm, left_hbm, right_hbm, out_ref,
    field, direct, left, right, coef_h, coef_l, left_h, left_l, right_h, right_l,
    part, buf1, sums, buf2, xbuf, rbuf, obuf, source, chosen_ref,
    field_sem, direct_sem, left_sem, right_sem,
    s1s, s1r, s2s, s2r, s3s, s3r, s4s, s4r, s5s, s5r, s6s, s6r,
):
    tables = gate_tables(nf)
    panels, slots, rows, width = right.shape
    pair = part.shape[1]
    virtual = pair // 2
    vp = virtual // nf
    blocks = rows // LANES
    np_ = 2 * ny
    tiles = np_ // blocks
    me = lax.axis_index("freq")
    q = lax.axis_index("panel")
    y, c = q // 2, q % 2
    partner = {"panel": y * 2 + 1 - c}
    ypeer = [{"panel": ((y + d) % ny) * 2 + c} for d in range(ny)]
    fpeer = [{"freq": (me + d) % nf} for d in range(nf)]
    MESH = pl.DeviceIdType.MESH

    loads_a, loads_b, loads_c = [], [], []
    for p in range(panels):
        cols = pl.ds(p * rows, rows)
        loads_a.append(pltpu.make_async_copy(field_hbm.at[:, :, cols], field.at[p], field_sem.at[p]))
        loads_a.append(pltpu.make_async_copy(left_hbm.at[:, cols, :], left.at[p], left_sem.at[p]))
        loads_b.append(pltpu.make_async_copy(right_hbm.at[p], right.at[p], right_sem.at[p]))
        loads_c.append(pltpu.make_async_copy(direct_hbm.at[:, :, cols], direct.at[p], direct_sem.at[p]))
    for copy in loads_a + loads_b + loads_c:
        copy.start()

    barrier = pltpu.get_barrier_semaphore()
    for dev in [partner] + ypeer[1:] + fpeer[1:]:
        pl.semaphore_signal(barrier, inc=1, device_id=dev, device_id_type=MESH)

    def slot_of(p, j):
        slot = jnp.int32(slots)
        for s in range(slots):
            slot = jnp.where(tile_ref[p, s] == j, jnp.int32(s), slot)
        return slot

    zero = jnp.zeros((pair, width), BF16)
    for p in range(panels):
        coef_h[p, slots] = zero
        coef_l[p, slots] = zero
        left_h[p, slots] = zero[:rows]
        left_l[p, slots] = zero[:rows]

    for p in range(panels):
        loads_a[2 * p].wait()
        loads_a[2 * p + 1].wait()
        fh, fl = split(field[p].reshape(pair, rows))
        fcat = lanes(fh, fh, fl)
        for s in range(0, slots, 2):
            halves = []
            for i in range(2):
                h, l = split(left[p, s + i])
                left_h[p, s + i] = h
                left_l[p, s + i] = l
                halves.append(jnp.concatenate([h, l, h], axis=0))
            products = mxu(fcat, lanes(*halves), NN)
            for i in range(2):
                h, l = split(pair_coef(products[:, i * width : (i + 1) * width]))
                coef_h[p, s + i] = h
                coef_l[p, s + i] = l
    for p in range(panels):
        loads_b[p].wait()
        for s in range(slots):
            h, l = split(right[p, s])
            right_h[p, s] = h
            right_l[p, s] = l

    def send(src, dst, ssem, rsem, device):
        copy = pltpu.make_async_remote_copy(
            src_ref=src, dst_ref=dst, send_sem=ssem, recv_sem=rsem, device_id=device, device_id_type=MESH
        )
        copy.start()
        return copy

    def block(yy, cc, ch):
        return ch * np_ + yy * 2 + cc

    order = list(range(1, ny)) + [0]
    c1 = [[None] * ny for _ in range(chunks)]
    c2 = [[None] * ny for _ in range(chunks)]
    c3 = [[None] * nf for _ in range(chunks)]
    c4 = [[None] * nf for _ in range(chunks)]
    c5 = [[None] * ny for _ in range(chunks)]
    c6 = [[None] * ny for _ in range(chunks)]

    def stage_adjoint(ch):
        for j in range(ch * tiles, (ch + 1) * tiles):
            ins, outs = [], []
            for p in range(panels):
                slot = slot_of(p, j)
                real = jnp.minimum(slot, slots - 1)
                h, l = coef_h[p, slot], coef_l[p, slot]
                rh, rl = right_h[p, real], right_l[p, real]
                ins += [h, l, h]
                outs += [rh, rh, rl]
            tile = mxu(lanes(*ins), lanes(*outs), NT_DIMS)
            for b in range(blocks):
                part[j * blocks + b] = tile[:, b * LANES : (b + 1) * LANES]
        if ch == 0:
            pl.semaphore_wait(barrier, 1 + (ny - 1) + (nf - 1))
        for d in order:
            c1[ch][d] = send(
                part.at[block((y + d) % ny, 1 - c, ch)], buf1.at[ch, d], s1s.at[ch, d], s1r.at[ch, d], partner
            )

    def stage_sum(ch):
        for d in order:
            c1[ch][d].wait_recv()
            sums[ch, d] = part[block((y + d) % ny, c, ch)] + buf1[ch, d]
            if d:
                c2[ch][d] = send(sums.at[ch, d], buf2.at[ch, d - 1], s2s.at[ch, d], s2r.at[ch, d], ypeer[d])

    def stage_out(ch):
        total = sums[ch, 0]
        for d in range(1, ny):
            c2[ch][d].wait_recv()
            total = total + buf2[ch, d - 1]
        if vp % 8 == 0:
            xbuf[ch] = total.reshape(2, nf, vp, LANES)
        else:
            for k in range(2 * nf):
                xbuf[ch, k // nf, k % nf] = total[k * vp : (k + 1) * vp]
        for d in range(1, nf):
            to = (me + d) % nf
            c3[ch][d] = send(xbuf.at[ch, :, to], rbuf.at[ch, me], s3s.at[ch, d], s3r.at[ch, d], fpeer[d])
        rbuf[ch, me] = xbuf[ch, :, me]

    def stage_gate(ch):
        at = block(y, c, ch)
        mark = onset_ref[:, pl.ds(pl.multiple_of(at * LANES, LANES), LANES)]
        cos, sin = unit(mark)
        for d in range(1, nf):
            c3[ch][d].wait_recv()
        xr = [rbuf[ch, f, 0] for f in range(nf)]
        xi = [rbuf[ch, f, 1] for f in range(nf)]
        br, bi = gate(xr, xi, cos, sin, mark.astype(F32), tables)
        for f in range(nf):
            obuf[ch, f, 0] = br[f]
            obuf[ch, f, 1] = bi[f]
        for d in range(1, nf):
            to = (me + d) % nf
            c4[ch][d] = send(obuf.at[ch, to], source.at[at, :, me], s4s.at[ch, d], s4r.at[ch, d], fpeer[d])
        source[at, :, me] = obuf[ch, me]

    def stage_back(ch):
        for d in range(1, nf):
            c4[ch][d].wait_recv()
        at = source.at[block(y, c, ch)]
        for d in range(1, ny):
            c5[ch][d] = send(at, at, s5s.at[ch, d], s5r.at[ch, d], ypeer[d])
        c6[ch][0] = send(at, at, s6s.at[ch, 0], s6r.at[ch, 0], partner)

    def stage_pass(ch):
        for d in range(1, ny):
            c5[ch][d].wait_recv()
            at = source.at[block((y + ny - d) % ny, c, ch)]
            c6[ch][d] = send(at, at, s6s.at[ch, d], s6r.at[ch, d], partner)

    def load_block(b):
        if vp % 8 == 0:
            return source[b].reshape(pair, LANES)
        for k in range(2 * nf):
            chosen_ref[k * vp : (k + 1) * vp, :] = source[b, k // nf, k % nf]
        return chosen_ref[...]

    def forward(ch, d):
        c6[ch][d].wait_recv()
        j = ch * tiles + (y + ny - d) % ny
        h, l = split(lanes(*[load_block(j * blocks + b) for b in range(blocks)]))
        at = [slot_of(p, j) for p in range(panels)]
        real = [jnp.minimum(a, slots - 1) for a in at]
        rh = lanes(*[right_h[p, real[p]] for p in range(panels)])
        rl = lanes(*[right_l[p, real[p]] for p in range(panels)])
        products = mxu(lanes(h, h, l), jnp.concatenate([rh, rl, rh], axis=0), NN)
        for p in range(panels):
            if ch == 0 and d == 0:
                loads_c[p].wait()
            ph, plow = split(pair_coef(products[:, p * width : (p + 1) * width]))
            lh, ll = left_h[p, at[p]], left_l[p, at[p]]
            total = mxu(lanes(ph, ph, plow), lanes(lh, ll, lh), NT_DIMS)
            done = direct[p] - total.reshape(2, virtual, rows)
            if ch == chunks - 1 and d == ny - 1:
                out_ref[:, :, p * rows : (p + 1) * rows] = done
            else:
                direct[p] = done

    def stage_own(ch):
        forward(ch, 0)

    def stage_forward(ch):
        for d in range(1, ny):
            forward(ch, d)

    assert blocks == 2
    for ch in range(chunks):
        stage_adjoint(ch)
        if ch:
            stage_sum(ch - 1)
    stage_sum(chunks - 1)
    stages = [(stage_gate, 2), (stage_out, 0), (stage_back, 3), (stage_pass, 5), (stage_forward, 6), (stage_own, 4)]
    for step in range(chunks + 6):
        for stage, lag in stages:
            if 0 <= step - lag < chunks:
                stage(step - lag)
    for group in (c1, c2, c3, c4, c5, c6):
        for ch in range(chunks):
            for copy in group[ch]:
                if copy is not None:
                    copy.wait_send()


def shards(nf, npanel, wavefield, direct, left_factors, right_factors, tile_src, onset):
    panels, slots = tile_src.shape
    rows, width = right_factors.shape[3:]
    virtual = wavefield.shape[2]
    blocks = SRC_TILES * rows // LANES
    chunks = blocks // npanel
    ny = npanel // 2
    vp = virtual // nf
    pair = 2 * virtual
    left = jnp.transpose(left_factors[0], (1, 0, 2))
    hbm = pl.BlockSpec(memory_space=pl.ANY)
    dma = lambda n: [pltpu.SemaphoreType.DMA((chunks, n))] * 2
    split_buf = lambda n, r: [pltpu.VMEM((panels, n, r, width), BF16)] * 2
    out = pl.pallas_call(
        functools.partial(marchenko_kernel, nf, ny, chunks),
        in_specs=[
            pl.BlockSpec(memory_space=pltpu.SMEM), pl.BlockSpec(memory_space=pltpu.VMEM), hbm, hbm, hbm, hbm,
        ],
        out_specs=pl.BlockSpec(memory_space=pltpu.VMEM),
        out_shape=pltpu.VMEM(direct.shape[1:], F32),
        scratch_shapes=[
            pltpu.VMEM((panels, 2, virtual, rows), F32),
            pltpu.VMEM((panels, 2, virtual, rows), F32),
            pltpu.VMEM((panels, slots, rows, width), F32),
            pltpu.VMEM((panels, slots, rows, width), F32),
            *split_buf(slots + 1, pair),
            *split_buf(slots + 1, rows),
            *split_buf(slots, rows),
            pltpu.VMEM((blocks, pair, LANES), F32),
            pltpu.VMEM((chunks, ny, pair, LANES), F32),
            pltpu.VMEM((chunks, ny, pair, LANES), F32),
            pltpu.VMEM((chunks, ny - 1, pair, LANES), F32),
            pltpu.VMEM((chunks, 2, nf, vp, LANES), F32),
            pltpu.VMEM((chunks, nf, 2, vp, LANES), F32),
            pltpu.VMEM((chunks, nf, 2, vp, LANES), F32),
            pltpu.VMEM((blocks, 2, nf, vp, LANES), F32),
            pltpu.VMEM((pair, LANES), F32),
            *[pltpu.SemaphoreType.DMA((panels,))] * 4,
            *dma(ny), *dma(ny), *dma(nf), *dma(nf), *dma(ny), *dma(ny),
        ],
        compiler_params=pltpu.CompilerParams(collective_id=0, has_side_effects=True),
        name="marchenko",
    )(tile_src, onset, wavefield[0], direct[0], left, right_factors[0])
    return out[None]


def solution(mesh):
    in_specs = (
        P("freq", None, None, "panel"),
        P("freq", None, None, "panel"),
        P("freq", "panel", None, None),
        P("freq", "panel", None, None, None),
        P("panel", None),
        P("freq", None),
    )
    out_specs = P("freq", None, None, "panel")
    body = functools.partial(shards, mesh.shape["freq"], mesh.shape["panel"])
    return jax.shard_map(body, mesh=mesh, in_specs=in_specs, out_specs=out_specs, check_vma=False)
```
